768 devices in a mesh: rows: 32 (over y, z_hi, core), feat: 24 (over x, z_lo).
Axes of the slice: x: 4, y: 8, z: 12 (z_hi: 2, z_lo: 6; z = z_hi * 6 + z_lo), core: 2. Of those that a mesh axis runs over, the one named last changes fastest.
Arguments:
- features: bfloat16 [393216, 512], P(('rows', 'feat')), may hold values from -6 to 6
- weight: bfloat16 [512, 512], replicated, may hold values from -0.25 to 0.25
- layer_bias: float32 [512], replicated, may hold values from -3 to 3
- block_cols: int32 [3072, 6], P(('rows', 'feat')), may hold values from 0 to 3071, as said below
- neighbours: int32 [393216, 30], P(('rows', 'feat')), may hold values from 0 to 767
- row_counts: int32 [393216], P(('rows', 'feat')), may hold values from 1 to 30
- out_grad: bfloat16 [393216, 512], P(('rows', 'feat')), may hold values from -6 to 6
Outputs:
- hidden: bfloat16 [393216, 512], P(('rows', 'feat'))
- input_grad: bfloat16 [393216, 512], P(('rows', 'feat'))
- weight_grad: float32 [512, 512], P('rows')
- bias_grad: float32 [512], P('rows')
The draws below stay inside these ranges and needn't reach their ends.
Inputs may be any that keep to these rules, and one draw needn't show every extreme that they name: `block_cols`: block row t is node rows 128 * t to 128 * t + 127. With g = (t // 4) * 4: slot 0 is t itself, slot 1 lies in tiles g - 4 to g - 1, slot 2 in tiles g + 4 to g + 2 * 4 - 1, and every slot in tiles g - 4 to g + 2 * 4 - 1, all taken modulo 3072. `neighbours`: entries at positions row_counts or later are unused.
All inputs are finite; a program needn't handle non-finite values.
Results may differ from the reference program's by a relative error of at most 0.0095.
Values may be sent and summed in bfloat16 or wider, within the bound.
No kernel may reach another device: no remote copies, remote signals or barrier semaphores. Data moves between devices by JAX's collectives and lax.ppermute only.
A program may use at most 64 MiB of HBM per device.

```python
import math
import jax
import jax.numpy as jnp
from jax import lax

F = 512
K = 30
BLK = 128
MAXB = 6
TILE_DEV = 4
NTILES = 3072
NODES = 393216


def draw_block_cols(key, part):
    first_key, second_key, third_key = jax.random.split(key, 3)
    tile_ids = jnp.arange(NTILES, dtype=jnp.int32)
    group_start = tile_ids // TILE_DEV * TILE_DEV
    own_place = tile_ids - group_start + TILE_DEV
    lower_pick = jax.random.randint(first_key, (NTILES, 1), 0, TILE_DEV, dtype=jnp.int32)
    upper_pick = jax.random.randint(second_key, (NTILES, 1), 0, TILE_DEV, dtype=jnp.int32) + 2 * TILE_DEV
    other_pick = jax.random.randint(third_key, (NTILES, MAXB - 3), 0, 3 * TILE_DEV, dtype=jnp.int32)
    places = jnp.concatenate([own_place[:, None], lower_pick, upper_pick, other_pick], axis=1)
    return jnp.mod(group_start[:, None] - TILE_DEV + places, NTILES).astype(jnp.int32)


def touch_ends(values, rng, least, top_value):
    index_at = [jax.random.randint(jax.random.fold_in(rng, axis), (), 0, length) for axis, length in enumerate(values.shape)]
    longest = values.shape.index(max(values.shape))
    beside = index_at[:longest] + [(index_at[longest] + 1) % values.shape[longest]] + index_at[longest + 1:]
    return values.at[tuple(index_at)].set(least).at[tuple(beside)].set(top_value)


def steps_of(stream_key, extent, shards, low, high):
    def one(axis_at, parts):
        heights = jax.random.uniform(jax.random.fold_in(jax.random.fold_in(stream_key, 6), axis_at), (parts,), jnp.float32, low / len(shards), high / len(shards))
        return jnp.repeat(jnp.exp(heights), extent[axis_at] // parts).reshape((-1,) + (1,) * (len(extent) - axis_at - 1))

    gain = one(*shards[0])
    for cut in shards[1:]:
        gain = gain * one(*cut)
    return gain


def gaussian(stream_key, shape, deviation, limit, pieces=(), held_as=jnp.bfloat16):
    values = deviation * jax.random.normal(stream_key, shape, jnp.float32)
    if pieces:
        values = values * steps_of(stream_key, shape, pieces, -0.22, 0.18)
    return jnp.clip(values, -limit, limit).astype(held_as)


def setup_inputs(seed: int = 0) -> dict:
    seeds = jax.random.split(jax.random.key(seed), 8)
    features = gaussian(seeds[0], (NODES, F), 1.0, 6.0, ((0, 768),))
    weight = gaussian(seeds[1], (F, F), F ** -0.5, 0.25)
    layer_bias = gaussian(seeds[2], (F,), 0.5, 3.0, (), jnp.float32)
    block_cols = draw_block_cols(jax.random.fold_in(seeds[7], 71), 0)
    neighbours = touch_ends(jax.random.randint(seeds[4], (NODES, K), 0, MAXB * BLK), jax.random.fold_in(seeds[4], 1), 0, (MAXB * BLK) - 1).astype(jnp.int32)
    row_counts = touch_ends(jax.random.randint(seeds[5], (NODES,), 1, K + 1), jax.random.fold_in(seeds[5], 1), 1, K).astype(jnp.int32)
    out_grad = gaussian(seeds[6], (NODES, F), 1.0, 6.0, ((0, 768),))
    return dict(features=features, weight=weight, layer_bias=layer_bias, block_cols=block_cols, neighbours=neighbours, row_counts=row_counts, out_grad=out_grad)


def strip_counts(neighbours, row_counts, strip_width):
    columns = jnp.arange(strip_width, dtype=jnp.int32)
    slot_ids = jnp.arange(neighbours.shape[1], dtype=jnp.int32)
    live_slot = slot_ids[None, :] < row_counts[:, None]
    matches = (neighbours[:, :, None] == columns[None, None, :]) & live_slot[:, :, None]
    return lax.optimization_barrier(jnp.sum(matches.astype(jnp.int32), axis=1)).astype(jnp.bfloat16)

def reference(features, weight, layer_bias, block_cols, neighbours, row_counts, out_grad):
    feat_width = features.shape[1]
    tile_total = block_cols.shape[0]
    normaliser = 1.0 / math.sqrt(NODES)
    inverse_root = lax.rsqrt(1.0 + row_counts.astype(jnp.float32))[:, None]
    projected = jnp.dot(features, weight, preferred_element_type=jnp.float32)
    proj_scaled = (projected * inverse_root).astype(jnp.bfloat16)
    scaled_tiles = proj_scaled.reshape(tile_total, BLK, feat_width)
    nbr_tiles = neighbours.reshape(tile_total, BLK, K)
    count_tiles = row_counts.reshape(tile_total, BLK)

    def forward_tile(operands):
        tile_cols, tile_nbr, tile_cnt = operands
        count_strip = strip_counts(tile_nbr, tile_cnt, MAXB * BLK)
        sources = scaled_tiles[tile_cols.astype(jnp.int32)].reshape(MAXB * BLK, feat_width)
        return jnp.dot(count_strip, sources, preferred_element_type=jnp.float32)
    summed = lax.map(forward_tile, (block_cols, nbr_tiles, count_tiles)).reshape(NODES, feat_width)
    pre_activation = inverse_root * (summed + proj_scaled.astype(jnp.float32)) + layer_bias[None, :]
    sigmoid_gate = jax.nn.sigmoid(pre_activation)
    hidden = (pre_activation * sigmoid_gate).astype(jnp.bfloat16)
    grad_pre = out_grad.astype(jnp.float32) * sigmoid_gate * (1.0 + pre_activation * (1.0 - sigmoid_gate))
    grad_scaled = (grad_pre * inverse_root).astype(jnp.bfloat16)
    grad_tiles = grad_scaled.reshape(tile_total, BLK, feat_width)

    def backward_tile(carried, operands):
        tile_cols, tile_nbr, tile_cnt, tile_grad = operands
        count_strip = strip_counts(tile_nbr, tile_cnt, MAXB * BLK)
        contribution = lax.dot_general(count_strip, tile_grad, (((0,), (0,)), ((), ())), preferred_element_type=jnp.float32)
        contribution = contribution.reshape(MAXB, BLK, feat_width)
        return (carried.at[tile_cols.astype(jnp.int32)].add(contribution), None)
    initial = jnp.zeros((tile_total, BLK, feat_width), jnp.float32)
    gathered, _ = lax.scan(backward_tile, initial, (block_cols, nbr_tiles, count_tiles, grad_tiles))
    gathered = gathered.reshape(NODES, feat_width)
    grad_proj = (inverse_root * (gathered + grad_scaled.astype(jnp.float32))).astype(jnp.bfloat16)
    input_grad = lax.dot_general(grad_proj, weight, (((1,), (1,)), ((), ())), preferred_element_type=jnp.float32).astype(jnp.bfloat16)
    weight_grad = lax.dot_general(features, grad_proj, (((0,), (0,)), ((), ())), preferred_element_type=jnp.float32) * normaliser
    bias_grad = lax.optimization_barrier(jnp.sum(grad_pre, axis=0)) * normaliser
    return (hidden, input_grad, weight_grad, bias_grad)
```

```python
import math

import jax
import jax.numpy as jnp
from jax import lax
from jax.experimental import pallas as pl
from jax.experimental.pallas import tpu as pltpu
from jax.sharding import Mesh
from jax.sharding import PartitionSpec as P

AXES = ("y", "zh", "core", "x", "zl")
SIZES = (8, 2, 2, 4, 6)
NODE = AXES
BITS = 5
f32 = jnp.float32
bf16 = jnp.bfloat16


def permute(array, axes, route):
    peers = lax.axis_size(axes)
    return lax.ppermute(array, axes, [(i, route(i) % peers) for i in range(peers)])


def rows_dot(a, b):
    return jnp.dot(a, b, preferred_element_type=f32)


def transposed_dot(a, b):
    return lax.dot_general(a, b, (((0,), (0,)), ((), ())), preferred_element_type=f32)


def adjacency_kernel(slot_ref, nbr_ref, cnt_ref, adj_ref, adjt_ref):
    tile = pl.program_id(0)
    rows, width = nbr_ref.shape
    slots = slot_ref.shape[1]
    tiles = adj_ref.shape[1] // rows
    own_first = tiles // 3
    nbr = nbr_ref[...]
    live = lax.broadcasted_iota(jnp.int32, nbr.shape, 1) < cnt_ref[...]
    low = jnp.bitwise_and(nbr, rows - 1)
    shift = BITS * lax.shift_right_logical(nbr, rows.bit_length() - 1)
    step = jnp.where(live, lax.shift_left(jnp.ones_like(nbr), shift), 0)
    lane = lax.broadcasted_iota(jnp.int32, (rows, rows), 1)
    packed = jnp.zeros((rows, rows), jnp.int32)
    for k in range(width):
        packed += jnp.where(lane == low[:, k : k + 1], step[:, k : k + 1], 0)
    adj_ref[...] = jnp.zeros_like(adj_ref)
    row = lax.broadcasted_iota(jnp.int32, (rows, rows), 0)
    own = pl.ds(pl.multiple_of((own_first + tile) * rows, rows), rows)
    adj_ref[:, own] = (row == lane).astype(f32).astype(bf16)
    for s in range(slots):
        counts = jnp.bitwise_and(lax.shift_right_logical(packed, BITS * s), 2**BITS - 1)
        place = pl.ds(pl.multiple_of(slot_ref[tile, s] * rows, rows), rows)
        adj_ref[:, place] += counts.astype(f32).astype(bf16)
    adjt_ref[...] = adj_ref[...].T


def build_adjacency(local_slot, neighbours, counts):
    tiles, slots = local_slot.shape
    nodes, width = neighbours.shape
    rows = nodes // tiles
    window = 3 * nodes
    return pl.pallas_call(
        adjacency_kernel,
        grid=(tiles,),
        in_specs=[
            pl.BlockSpec(memory_space=pltpu.SMEM),
            pl.BlockSpec((rows, width), lambda t: (t, 0)),
            pl.BlockSpec((rows, 1), lambda t: (t, 0)),
        ],
        out_specs=[
            pl.BlockSpec((rows, window), lambda t: (t, 0)),
            pl.BlockSpec((window, rows), lambda t: (0, t)),
        ],
        out_shape=[
            jax.ShapeDtypeStruct((nodes, window), bf16),
            jax.ShapeDtypeStruct((window, nodes), bf16),
        ],
        cost_estimate=pl.CostEstimate(flops=10**9, bytes_accessed=8 * 10**6, transcendentals=0),
        name="adjacency",
    )(local_slot, neighbours, counts)


def middle_kernel(
    core_ref, adj, adjt, own, left, right, weight, bias, root, grad,
    hidden, wsend, wkeep, part_left, part_right, part_own, agg_s, scaled_s, pre_s,
):
    nodes, width = own.shape
    rows = 128
    for first in range(0, nodes, rows):
        r = pl.ds(first, rows)
        agg = rows_dot(adj[r, 0:nodes], left[...])
        agg += rows_dot(adj[r, nodes : 2 * nodes], own[...])
        agg += rows_dot(adj[r, 2 * nodes : 3 * nodes], right[...])
        agg = agg.astype(bf16)
        agg_s[r, :] = agg
        pre = root[r, :] * rows_dot(agg, weight[...]) + bias[...]
        gate = jax.nn.sigmoid(pre)
        hidden[r, :] = (pre * gate).astype(bf16)
        grad_pre = grad[r, :].astype(f32) * gate * (1.0 + pre * (1.0 - gate))
        pre_s[r, :] = grad_pre.astype(bf16)
        scaled_s[r, :] = (grad_pre * root[r, :]).astype(bf16)
    scaled = scaled_s[...]
    core = core_ref[0]
    ones = jnp.ones((nodes, 128), bf16)
    wgrad = transposed_dot(agg_s[...], scaled).astype(bf16)
    bgrad = transposed_dot(pre_s[...], ones).astype(bf16)
    share = 16
    for chunk in range(width // share):
        outer, side = divmod(chunk, 2)
        band = slice(chunk * share, (chunk + 1) * share)
        place = pl.ds(outer * share, share)

        @pl.when(core == side)
        def _():
            wkeep[place, 0:width] = wgrad[band]
            wkeep[place, width : width + 128] = bgrad[band]

        @pl.when(core != side)
        def _():
            wsend[place, 0:width] = wgrad[band]
            wsend[place, width : width + 128] = bgrad[band]

    part_left[...] = rows_dot(adjt[0:nodes, :], scaled).astype(bf16)
    part_right[...] = rows_dot(adjt[2 * nodes : 3 * nodes, :], scaled).astype(bf16)
    part_own[...] = rows_dot(adjt[nodes : 2 * nodes, :], scaled)


def middle(core, adj, adjt, own, left, right, weight, bias, root, grad):
    nodes, width = own.shape
    half = jax.ShapeDtypeStruct((width // 2, width + 128), bf16)
    square = jax.ShapeDtypeStruct((nodes, width), bf16)
    vmem = pl.BlockSpec(memory_space=pltpu.VMEM)
    return pl.pallas_call(
        middle_kernel,
        in_specs=[pl.BlockSpec(memory_space=pltpu.SMEM)] + [vmem] * 9,
        out_specs=[vmem] * 6,
        out_shape=[square, half, half, square, square, jax.ShapeDtypeStruct((nodes, width), f32)],
        scratch_shapes=[pltpu.VMEM((nodes, width), bf16)] * 3,
        cost_estimate=pl.CostEstimate(flops=2 * 10**9, bytes_accessed=10**7, transcendentals=0),
        name="middle",
    )(core, adj, adjt, own, left, right, weight, bias, root, grad)


def final_kernel(part_own, from_left, from_right, root, weight, out):
    nodes = out.shape[0]
    rows = 128
    for first in range(0, nodes, rows):
        r = pl.ds(first, rows)
        total = part_own[r, :] + from_left[r, :].astype(f32) + from_right[r, :].astype(f32)
        grad_proj = (root[r, :] * total).astype(bf16)
        out[r, :] = lax.dot_general(
            grad_proj, weight[...], (((1,), (1,)), ((), ())), preferred_element_type=f32
        ).astype(bf16)


def final(part_own, from_left, from_right, root, weight):
    vmem = pl.BlockSpec(memory_space=pltpu.VMEM)
    return pl.pallas_call(
        final_kernel,
        in_specs=[vmem] * 5,
        out_specs=vmem,
        out_shape=jax.ShapeDtypeStruct(part_own.shape, bf16),
        cost_estimate=pl.CostEstimate(flops=10**8, bytes_accessed=10**6, transcendentals=0),
        name="final",
    )(part_own, from_left, from_right, root, weight)


def local(features, weight, layer_bias, block_cols, neighbours, row_counts, out_grad):
    nodes, width = features.shape
    tile_count = block_cols.shape[0]
    devices = lax.axis_size(NODE)
    all_tiles = tile_count * devices
    normaliser = 1.0 / math.sqrt(nodes * devices)
    window_start = (lax.axis_index(NODE) - 1) * tile_count
    local_slot = jnp.mod(block_cols - window_start, all_tiles)
    counts = row_counts[:, None]
    root = lax.rsqrt(1.0 + counts.astype(f32))
    own = (features.astype(f32) * root).astype(bf16)
    left = permute(own, NODE, lambda i: i + 1)
    right = permute(own, NODE, lambda i: i - 1)
    adj, adjt = build_adjacency(local_slot, neighbours, counts)
    core = lax.axis_index("core").astype(jnp.int32).reshape(1)
    hidden, wsend, wkeep, part_left, part_right, part_own = middle(
        core, adj, adjt, own, left, right, weight, layer_bias[None, :], root, out_grad
    )
    got = permute(wsend, "core", lambda i: i ^ 1)
    from_right = permute(part_left, NODE, lambda i: i - 1)
    from_left = permute(part_right, NODE, lambda i: i + 1)

    ny, nzh = lax.axis_size("y"), lax.axis_size("zh")
    share = width // (ny * nzh * lax.axis_size("core"))
    chip = (wkeep.astype(f32) + got.astype(f32)).astype(bf16)
    chip = chip.reshape(ny, nzh * share, width + 128)
    column = jnp.sum(lax.all_to_all(chip, "y", 0, 0).astype(f32), axis=0)
    high = lax.axis_index("zh")
    kept = jnp.where(high == 0, column[:share], column[share:])
    sent = jnp.where(high == 0, column[share:], column[:share]).astype(bf16)
    pair = kept + permute(sent, ("zh", "zl"), lambda i: -1 - i).astype(f32)
    spread = lax.axis_size(("x", "zl"))
    every = jnp.broadcast_to(pair.astype(bf16)[None], (spread, share, width + 128))
    total = jnp.sum(lax.all_to_all(every, ("x", "zl"), 0, 0).astype(f32), axis=0) * normaliser

    input_grad = final(part_own, from_left, from_right, root, weight)
    return (hidden, input_grad, total[:, :width], total[:, width])


def solution(mesh):
    wide = Mesh(mesh.devices.reshape(SIZES), AXES)
    row = P(NODE, None)
    in_specs = (row, P(), P(), row, row, P(NODE), row)
    shares = ("y", "zh", "core")
    out_specs = (row, row, P(shares, None), P(shares))
    return jax.shard_map(local, mesh=wide, in_specs=in_specs, out_specs=out_specs, check_vma=False)
```

```python
import math

import jax
import jax.numpy as jnp
from jax import lax
from jax.experimental import pallas as pl
from jax.experimental.pallas import tpu as pltpu
from jax.sharding import Mesh
from jax.sharding import PartitionSpec as P

AXES = ("y", "zh", "core", "x", "zl")
SIZES = (8, 2, 2, 4, 6)
NODE = AXES
BITS = 5
VMEM_LIMIT = 20 * 2**20
f32 = jnp.float32
bf16 = jnp.bfloat16


def permute(array, axes, route):
    peers = lax.axis_size(axes)
    return lax.ppermute(array, axes, [(i, route(i) % peers) for i in range(peers)])


def rows_dot(a, b):
    return jnp.dot(a, b, preferred_element_type=f32)


def transposed_dot(a, b):
    return lax.dot_general(a, b, (((0,), (0,)), ((), ())), preferred_element_type=f32)


def adjacency_kernel(slot_ref, nbr_ref, cnt_ref, adj_ref, adjt_ref):
    tile = pl.program_id(0)
    rows, width = nbr_ref.shape
    slots = slot_ref.shape[1]
    tiles = adj_ref.shape[1] // rows
    own_first = tiles // 3
    nbr = nbr_ref[...]
    live = lax.broadcasted_iota(jnp.int32, nbr.shape, 1) < cnt_ref[...]
    low = jnp.bitwise_and(nbr, rows - 1)
    shift = BITS * lax.shift_right_logical(nbr, rows.bit_length() - 1)
    step = jnp.where(live, lax.shift_left(jnp.ones_like(nbr), shift), 0)
    lane = lax.broadcasted_iota(jnp.int32, (rows, rows), 1)
    packed = jnp.zeros((rows, rows), jnp.int32)
    for k in range(width):
        packed += jnp.where(lane == low[:, k : k + 1], step[:, k : k + 1], 0)
    adj_ref[...] = jnp.zeros_like(adj_ref)
    row = lax.broadcasted_iota(jnp.int32, (rows, rows), 0)
    own = pl.ds(pl.multiple_of((own_first + tile) * rows, rows), rows)
    adj_ref[:, own] = (row == lane).astype(f32).astype(bf16)
    for s in range(slots):
        counts = jnp.bitwise_and(lax.shift_right_logical(packed, BITS * s), 2**BITS - 1)
        place = pl.ds(pl.multiple_of(slot_ref[tile, s] * rows, rows), rows)
        adj_ref[:, place] += counts.astype(f32).astype(bf16)
    adjt_ref[...] = adj_ref[...].T


def build_adjacency(local_slot, neighbours, counts):
    tiles, slots = local_slot.shape
    nodes, width = neighbours.shape
    rows = nodes // tiles
    window = 3 * nodes
    return pl.pallas_call(
        adjacency_kernel,
        grid=(tiles,),
        in_specs=[
            pl.BlockSpec(memory_space=pltpu.SMEM),
            pl.BlockSpec((rows, width), lambda t: (t, 0)),
            pl.BlockSpec((rows, 1), lambda t: (t, 0)),
        ],
        out_specs=[
            pl.BlockSpec((rows, window), lambda t: (t, 0)),
            pl.BlockSpec((window, rows), lambda t: (0, t)),
        ],
        out_shape=[
            jax.ShapeDtypeStruct((nodes, window), bf16),
            jax.ShapeDtypeStruct((window, nodes), bf16),
        ],
        cost_estimate=pl.CostEstimate(flops=10**9, bytes_accessed=8 * 10**6, transcendentals=0),
        compiler_params=pltpu.CompilerParams(vmem_limit_bytes=VMEM_LIMIT),
        name="adjacency",
    )(local_slot, neighbours, counts)


def forward_kernel(
    core_ref, adj, own, left, right, weight, bias, root, grad,
    hidden, wsend, wkeep, scaled, agg_s, pre_s,
):
    nodes, width = own.shape
    rows = 128
    for first in range(0, nodes, rows):
        r = pl.ds(first, rows)
        agg = rows_dot(adj[r, 0:nodes], left[...])
        agg += rows_dot(adj[r, nodes : 2 * nodes], own[...])
        agg += rows_dot(adj[r, 2 * nodes : 3 * nodes], right[...])
        agg = agg.astype(bf16)
        agg_s[r, :] = agg
        pre = root[r, :] * rows_dot(agg, weight[...]) + bias[...]
        gate = jax.nn.sigmoid(pre)
        hidden[r, :] = (pre * gate).astype(bf16)
        grad_pre = grad[r, :].astype(f32) * gate * (1.0 + pre * (1.0 - gate))
        pre_s[r, :] = grad_pre.astype(bf16)
        scaled[r, :] = (grad_pre * root[r, :]).astype(bf16)
    core = core_ref[0]
    ones = jnp.ones((nodes, 128), bf16)
    wgrad = transposed_dot(agg_s[...], scaled[...]).astype(bf16)
    bgrad = transposed_dot(pre_s[...], ones).astype(bf16)
    share = 16
    for chunk in range(width // share):
        outer, side = divmod(chunk, 2)
        band = slice(chunk * share, (chunk + 1) * share)
        place = pl.ds(outer * share, share)

        @pl.when(core == side)
        def _():
            wkeep[place, 0:width] = wgrad[band]
            wkeep[place, width : width + 128] = bgrad[band]

        @pl.when(core != side)
        def _():
            wsend[place, 0:width] = wgrad[band]
            wsend[place, width : width + 128] = bgrad[band]


def forward(core, adj, own, left, right, weight, bias, root, grad):
    nodes, width = own.shape
    half = jax.ShapeDtypeStruct((width // 2, width + 128), bf16)
    square = jax.ShapeDtypeStruct((nodes, width), bf16)
    vmem = pl.BlockSpec(memory_space=pltpu.VMEM)
    return pl.pallas_call(
        forward_kernel,
        in_specs=[pl.BlockSpec(memory_space=pltpu.SMEM)] + [vmem] * 8,
        out_specs=[vmem] * 4,
        out_shape=[square, half, half, square],
        scratch_shapes=[pltpu.VMEM((nodes, width), bf16)] * 2,
        compiler_params=pltpu.CompilerParams(vmem_limit_bytes=VMEM_LIMIT),
        cost_estimate=pl.CostEstimate(flops=10**9, bytes_accessed=10**7, transcendentals=0),
        name="forward",
    )(core, adj, own, left, right, weight, bias, root, grad)


def parts_kernel(adjt, scaled, part_left, part_right, part_own):
    nodes = scaled.shape[0]
    for first in range(0, nodes, 128):
        r = pl.ds(first, 128)
        part_left[r, :] = rows_dot(adjt[first : first + 128, :], scaled[...]).astype(bf16)
    for first in range(0, nodes, 128):
        r = pl.ds(first, 128)
        low = 2 * nodes + first
        part_right[r, :] = rows_dot(adjt[low : low + 128, :], scaled[...]).astype(bf16)
    for first in range(0, nodes, 128):
        r = pl.ds(first, 128)
        low = nodes + first
        part_own[r, :] = rows_dot(adjt[low : low + 128, :], scaled[...])


def parts(adjt, scaled):
    nodes, width = scaled.shape
    square = jax.ShapeDtypeStruct((nodes, width), bf16)
    vmem = pl.BlockSpec(memory_space=pltpu.VMEM)
    return pl.pallas_call(
        parts_kernel,
        in_specs=[vmem] * 2,
        out_specs=[vmem] * 3,
        out_shape=[square, square, jax.ShapeDtypeStruct((nodes, width), f32)],
        compiler_params=pltpu.CompilerParams(vmem_limit_bytes=VMEM_LIMIT),
        cost_estimate=pl.CostEstimate(flops=10**9, bytes_accessed=10**7, transcendentals=0),
        name="parts",
    )(adjt, scaled)


def final_kernel(part_own, from_left, from_right, root, weight, out):
    nodes = out.shape[0]
    rows = 128
    for first in range(0, nodes, rows):
        r = pl.ds(first, rows)
        total = part_own[r, :] + from_left[r, :].astype(f32) + from_right[r, :].astype(f32)
        grad_proj = (root[r, :] * total).astype(bf16)
        out[r, :] = lax.dot_general(
            grad_proj, weight[...], (((1,), (1,)), ((), ())), preferred_element_type=f32
        ).astype(bf16)


def final(part_own, from_left, from_right, root, weight):
    vmem = pl.BlockSpec(memory_space=pltpu.VMEM)
    return pl.pallas_call(
        final_kernel,
        in_specs=[vmem] * 5,
        out_specs=vmem,
        out_shape=jax.ShapeDtypeStruct(part_own.shape, bf16),
        cost_estimate=pl.CostEstimate(flops=10**8, bytes_accessed=10**6, transcendentals=0),
        compiler_params=pltpu.CompilerParams(vmem_limit_bytes=VMEM_LIMIT),
        name="final",
    )(part_own, from_left, from_right, root, weight)


def local(features, weight, layer_bias, block_cols, neighbours, row_counts, out_grad):
    nodes, width = features.shape
    tile_count = block_cols.shape[0]
    devices = lax.axis_size(NODE)
    all_tiles = tile_count * devices
    normaliser = 1.0 / math.sqrt(nodes * devices)
    window_start = (lax.axis_index(NODE) - 1) * tile_count
    local_slot = jnp.mod(block_cols - window_start, all_tiles)
    counts = row_counts[:, None]
    root = lax.rsqrt(1.0 + counts.astype(f32))
    own = (features.astype(f32) * root).astype(bf16)
    left = permute(own, NODE, lambda i: i + 1)
    right = permute(own, NODE, lambda i: i - 1)
    adj, adjt = build_adjacency(local_slot, neighbours, counts)
    core = lax.axis_index("core").astype(jnp.int32).reshape(1)
    hidden, wsend, wkeep, scaled = forward(
        core, adj, own, left, right, weight, layer_bias[None, :], root, out_grad
    )
    got = permute(wsend, "core", lambda i: i ^ 1)
    part_left, part_right, part_own = parts(adjt, scaled)
    from_right = permute(part_left, NODE, lambda i: i - 1)
    from_left = permute(part_right, NODE, lambda i: i + 1)

    ny, nzh = lax.axis_size("y"), lax.axis_size("zh")
    share = width // (ny * nzh * lax.axis_size("core"))
    chip = (wkeep.astype(f32) + got.astype(f32)).astype(bf16)
    chip = chip.reshape(ny, nzh * share, width + 128)
    column = jnp.sum(lax.all_to_all(chip, "y", 0, 0).astype(f32), axis=0)
    high = lax.axis_index("zh")
    kept = jnp.where(high == 0, column[:share], column[share:])
    sent = jnp.where(high == 0, column[share:], column[:share]).astype(bf16)
    sent, from_left, from_right = lax.optimization_barrier((sent, from_left, from_right))
    pair = kept + permute(sent, ("zh", "zl"), lambda i: -1 - i).astype(f32)
    spread = lax.axis_size(("x", "zl"))
    every = jnp.broadcast_to(pair.astype(bf16)[None], (spread, share, width + 128))
    total = jnp.sum(lax.all_to_all(every, ("x", "zl"), 0, 0).astype(f32), axis=0) * normaliser

    input_grad = final(part_own, from_left, from_right, root, weight)
    return (hidden, input_grad, total[:, :width], total[:, width])


def solution(mesh):
    wide = Mesh(mesh.devices.reshape(SIZES), AXES)
    row = P(NODE, None)
    in_specs = (row, P(), P(), row, row, P(NODE), row)
    shares = ("y", "zh", "core")
    out_specs = (row, row, P(shares, None), P(shares))
    return jax.shard_map(local, mesh=wide, in_specs=in_specs, out_specs=out_specs, check_vma=False)
```

```python
import math

import jax
import jax.numpy as jnp
from jax import lax
from jax.experimental import pallas as pl
from jax.experimental.pallas import tpu as pltpu
from jax.sharding import Mesh
from jax.sharding import PartitionSpec as P

AXES = ("y", "zh", "core", "x", "zl")
SIZES = (8, 2, 2, 4, 6)
NODE = AXES
BITS = 5
VMEM_LIMIT = 20 * 2**20
f32 = jnp.float32
bf16 = jnp.bfloat16


def permute(array, axes, route):
    peers = lax.axis_size(axes)
    return lax.ppermute(array, axes, [(i, route(i) % peers) for i in range(peers)])


def near_partner(i):
    return i ^ 1


def far_partner(i):
    return i + 1 if i % 2 else i - 1


def rows_dot(a, b):
    return jnp.dot(a, b, preferred_element_type=f32)


def transposed_dot(a, b):
    return lax.dot_general(a, b, (((0,), (0,)), ((), ())), preferred_element_type=f32)


def adjacency_kernel(slot_ref, nbr_ref, cnt_ref, adj_ref, edge_ref, own_ref):
    tile = pl.program_id(0)
    rows, width = nbr_ref.shape
    slots = slot_ref.shape[1]
    tiles = adj_ref.shape[1] // rows
    own_first = tiles // 3
    nbr = nbr_ref[...]
    live = lax.broadcasted_iota(jnp.int32, nbr.shape, 1) < cnt_ref[...]
    low = jnp.bitwise_and(nbr, rows - 1)
    shift = BITS * lax.shift_right_logical(nbr, rows.bit_length() - 1)
    step = jnp.where(live, lax.shift_left(jnp.ones_like(nbr), shift), 0)
    lane = lax.broadcasted_iota(jnp.int32, (rows, rows), 1)
    packed = jnp.zeros((rows, rows), jnp.int32)
    for k in range(width):
        packed += jnp.where(lane == low[:, k : k + 1], step[:, k : k + 1], 0)
    adj_ref[...] = jnp.zeros_like(adj_ref)
    row = lax.broadcasted_iota(jnp.int32, (rows, rows), 0)
    own = pl.ds(pl.multiple_of((own_first + tile) * rows, rows), rows)
    adj_ref[:, own] = (row == lane).astype(f32).astype(bf16)
    for s in range(slots):
        counts = jnp.bitwise_and(lax.shift_right_logical(packed, BITS * s), 2**BITS - 1)
        place = pl.ds(pl.multiple_of(slot_ref[tile, s] * rows, rows), rows)
        adj_ref[:, place] += counts.astype(f32).astype(bf16)
    nodes = tiles // 3 * rows
    edge_ref[0:nodes, :] = adj_ref[:, 0:nodes].T
    edge_ref[nodes : 2 * nodes, :] = adj_ref[:, 2 * nodes : 3 * nodes].T
    own_ref[...] = adj_ref[:, nodes : 2 * nodes].T


def build_adjacency(local_slot, neighbours, counts):
    tiles, slots = local_slot.shape
    nodes, width = neighbours.shape
    rows = nodes // tiles
    window = 3 * nodes
    return pl.pallas_call(
        adjacency_kernel,
        grid=(tiles,),
        in_specs=[
            pl.BlockSpec(memory_space=pltpu.SMEM),
            pl.BlockSpec((rows, width), lambda t: (t, 0)),
            pl.BlockSpec((rows, 1), lambda t: (t, 0)),
        ],
        out_specs=[
            pl.BlockSpec((rows, window), lambda t: (t, 0)),
            pl.BlockSpec((2 * nodes, rows), lambda t: (0, t)),
            pl.BlockSpec((nodes, rows), lambda t: (0, t)),
        ],
        out_shape=[
            jax.ShapeDtypeStruct((nodes, window), bf16),
            jax.ShapeDtypeStruct((2 * nodes, nodes), bf16),
            jax.ShapeDtypeStruct((nodes, nodes), bf16),
        ],
        cost_estimate=pl.CostEstimate(flops=10**9, bytes_accessed=8 * 10**6, transcendentals=0),
        compiler_params=pltpu.CompilerParams(vmem_limit_bytes=VMEM_LIMIT),
        name="adjacency",
    )(local_slot, neighbours, counts)


def forward_kernel(
    core_ref, adj, own, near, far, weight, bias, root, grad,
    hidden, wsend, wkeep, scaled, agg_s, pre_s,
):
    nodes, width = own.shape
    rows = 128
    for first in range(0, nodes, rows):
        r = pl.ds(first, rows)
        agg = rows_dot(adj[r, 0:nodes], near[...])
        agg += rows_dot(adj[r, nodes : 2 * nodes], own[...])
        agg += rows_dot(adj[r, 2 * nodes : 3 * nodes], far[...])
        agg = agg.astype(bf16)
        agg_s[r, :] = agg
        pre = root[r, :] * rows_dot(agg, weight[...]) + bias[...]
        gate = jax.nn.sigmoid(pre)
        hidden[r, :] = (pre * gate).astype(bf16)
        grad_pre = grad[r, :].astype(f32) * gate * (1.0 + pre * (1.0 - gate))
        pre_s[r, :] = grad_pre.astype(bf16)
        scaled[r, :] = (grad_pre * root[r, :]).astype(bf16)
    core = core_ref[0]
    ones = jnp.ones((nodes, 128), bf16)
    wgrad = transposed_dot(agg_s[...], scaled[...]).astype(bf16)
    bgrad = transposed_dot(pre_s[...], ones).astype(bf16)
    share = 16
    for chunk in range(width // share):
        outer, side = divmod(chunk, 2)
        band = slice(chunk * share, (chunk + 1) * share)
        place = pl.ds(outer * share, share)

        @pl.when(core == side)
        def _():
            wkeep[place, 0:width] = wgrad[band]
            wkeep[place, width : width + 128] = bgrad[band]

        @pl.when(core != side)
        def _():
            wsend[place, 0:width] = wgrad[band]
            wsend[place, width : width + 128] = bgrad[band]


def forward(core, adj, own, near, far, weight, bias, root, grad):
    nodes, width = own.shape
    half = jax.ShapeDtypeStruct((width // 2, width + 128), bf16)
    square = jax.ShapeDtypeStruct((nodes, width), bf16)
    vmem = pl.BlockSpec(memory_space=pltpu.VMEM)
    return pl.pallas_call(
        forward_kernel,
        in_specs=[pl.BlockSpec(memory_space=pltpu.SMEM)] + [vmem] * 8,
        out_specs=[vmem] * 4,
        out_shape=[square, half, half, square],
        scratch_shapes=[pltpu.VMEM((nodes, width), bf16)] * 2,
        compiler_params=pltpu.CompilerParams(vmem_limit_bytes=VMEM_LIMIT),
        cost_estimate=pl.CostEstimate(flops=10**9, bytes_accessed=10**7, transcendentals=0),
        name="forward",
    )(core, adj, own, near, far, weight, bias, root, grad)


def parts_kernel(edge, scaled, part_near, part_far):
    nodes = scaled.shape[0]
    rows = 128
    for first in range(0, nodes, rows):
        part = rows_dot(edge[first : first + rows, :], scaled[...])
        part_near[first : first + rows, :] = part.astype(bf16)
        part = rows_dot(edge[nodes + first : nodes + first + rows, :], scaled[...])
        part_far[first : first + rows, :] = part.astype(bf16)


def parts(edge, scaled):
    square = jax.ShapeDtypeStruct(scaled.shape, bf16)
    vmem = pl.BlockSpec(memory_space=pltpu.VMEM)
    return pl.pallas_call(
        parts_kernel,
        in_specs=[vmem] * 2,
        out_specs=[vmem] * 2,
        out_shape=[square, square],
        compiler_params=pltpu.CompilerParams(vmem_limit_bytes=VMEM_LIMIT),
        cost_estimate=pl.CostEstimate(flops=10**8, bytes_accessed=10**6, transcendentals=0),
        name="parts",
    )(edge, scaled)


def spread_kernel(blocks, out):
    count = blocks.shape[0]
    total = blocks[0].astype(f32)
    for i in range(1, count):
        total += blocks[i].astype(f32)
    total = total.astype(bf16)
    copies, rows = out.shape[0], out.shape[1]
    each = copies * rows // blocks.shape[1]
    for i in range(copies):
        first = i // each * rows
        out[i] = total[first : first + rows]


def spread(blocks, pieces, copies):
    _, rows, width = blocks.shape
    vmem = pl.BlockSpec(memory_space=pltpu.VMEM)
    return pl.pallas_call(
        spread_kernel,
        in_specs=[vmem],
        out_specs=vmem,
        out_shape=jax.ShapeDtypeStruct((pieces * copies, rows // pieces, width), bf16),
        compiler_params=pltpu.CompilerParams(vmem_limit_bytes=VMEM_LIMIT),
        cost_estimate=pl.CostEstimate(flops=10**6, bytes_accessed=10**6, transcendentals=0),
        name="spread",
    )(blocks)


def last_sum_kernel(scale, blocks, out, bias):
    count, rows, width = blocks.shape
    total = blocks[0].astype(f32)
    for i in range(1, count):
        total += blocks[i].astype(f32)
    total = total * scale
    wide = out.shape[1]
    out[...] = total[:, 0:wide]
    column = total[:, wide:width]
    row = lax.broadcasted_iota(jnp.int32, column.shape, 0)
    lane = lax.broadcasted_iota(jnp.int32, column.shape, 1)
    flat = jnp.sum(jnp.where(row == lane, column, 0.0), axis=0, keepdims=True)
    bias[...] = flat[:, 0:rows]


def last_sum(blocks, scale):
    _, rows, width = blocks.shape
    vmem = pl.BlockSpec(memory_space=pltpu.VMEM)
    return pl.pallas_call(
        lambda *refs: last_sum_kernel(scale, *refs),
        in_specs=[vmem],
        out_specs=[vmem] * 2,
        out_shape=[
            jax.ShapeDtypeStruct((rows, width - 128), f32),
            jax.ShapeDtypeStruct((1, rows), f32),
        ],
        compiler_params=pltpu.CompilerParams(vmem_limit_bytes=VMEM_LIMIT),
        cost_estimate=pl.CostEstimate(flops=10**6, bytes_accessed=10**6, transcendentals=0),
        name="last_sum",
    )(blocks)


def own_part_kernel(adj, scaled, out):
    rows = 128
    for first in range(0, out.shape[0], rows):
        out[first : first + rows, :] = rows_dot(adj[first : first + rows, :], scaled[...])


def own_part(adj, scaled):
    vmem = pl.BlockSpec(memory_space=pltpu.VMEM)
    return pl.pallas_call(
        own_part_kernel,
        in_specs=[vmem] * 2,
        out_specs=vmem,
        out_shape=jax.ShapeDtypeStruct(scaled.shape, f32),
        compiler_params=pltpu.CompilerParams(vmem_limit_bytes=VMEM_LIMIT),
        cost_estimate=pl.CostEstimate(flops=10**12, bytes_accessed=10**9, transcendentals=0),
        name="own_part",
    )(adj, scaled)


def final_kernel(part_own, from_near, from_far, root, weight, out):
    nodes = out.shape[0]
    rows = 128
    for first in range(0, nodes, rows):
        r = pl.ds(first, rows)
        total = part_own[r, :] + from_near[r, :].astype(f32) + from_far[r, :].astype(f32)
        grad_proj = (root[r, :] * total).astype(bf16)
        out[r, :] = lax.dot_general(
            grad_proj, weight[...], (((1,), (1,)), ((), ())), preferred_element_type=f32
        ).astype(bf16)


def final(part_own, from_near, from_far, root, weight):
    vmem = pl.BlockSpec(memory_space=pltpu.VMEM)
    return pl.pallas_call(
        final_kernel,
        in_specs=[vmem] * 5,
        out_specs=vmem,
        out_shape=jax.ShapeDtypeStruct(part_own.shape, bf16),
        cost_estimate=pl.CostEstimate(flops=10**8, bytes_accessed=10**6, transcendentals=0),
        compiler_params=pltpu.CompilerParams(vmem_limit_bytes=VMEM_LIMIT),
        name="final",
    )(part_own, from_near, from_far, root, weight)


def local(features, weight, layer_bias, block_cols, neighbours, row_counts, out_grad):
    nodes, width = features.shape
    tile_count = block_cols.shape[0]
    devices = lax.axis_size(NODE)
    all_tiles = tile_count * devices
    normaliser = 1.0 / math.sqrt(nodes * devices)
    window_start = (lax.axis_index(NODE) - 1) * tile_count
    local_slot = jnp.mod(block_cols - window_start, all_tiles)
    group = local_slot // tile_count
    even = lax.axis_index(NODE) % 2 == 0
    local_slot = jnp.where(even, local_slot + 2 * (1 - group) * tile_count, local_slot)
    counts = row_counts[:, None]
    root = lax.rsqrt(1.0 + counts.astype(f32))
    own = (features.astype(f32) * root).astype(bf16)
    far = permute(own, NODE, far_partner)
    near = permute(own, NODE, near_partner)
    adj, edge, own_t = build_adjacency(local_slot, neighbours, counts)
    core = lax.axis_index("core").astype(jnp.int32).reshape(1)
    hidden, wsend, wkeep, scaled = forward(
        core, adj, own, near, far, weight, layer_bias[None, :], root, out_grad
    )
    got = permute(wsend, "core", lambda i: i ^ 1)
    part_near, part_far = parts(edge, scaled)
    from_far = permute(part_far, NODE, far_partner)
    from_near = permute(part_near, NODE, near_partner)
    ny, nx, nzh, nzl = (lax.axis_size(n) for n in ("y", "x", "zh", "zl"))
    chip = (wkeep.astype(f32) + got.astype(f32)).astype(bf16)
    blocks = lax.all_to_all(chip.reshape(ny, -1, width + 128), "y", 0, 0)
    blocks = lax.all_to_all(spread(blocks, nzh, nzl), ("zh", "zl"), 0, 0)
    part_own = own_part(own_t, scaled)
    blocks, part_own = lax.optimization_barrier((blocks, part_own))
    blocks = spread(blocks, 1, nx)
    blocks, from_near, from_far = lax.optimization_barrier((blocks, from_near, from_far))
    blocks = lax.all_to_all(blocks, "x", 0, 0)
    weight_grad, bias_grad = last_sum(blocks, normaliser)
    input_grad = final(part_own, from_near, from_far, root, weight)
    return (hidden, input_grad, weight_grad, bias_grad[0])


def solution(mesh):
    wide = Mesh(mesh.devices.reshape(SIZES), AXES)
    row = P(NODE, None)
    in_specs = (row, P(), P(), row, row, P(NODE), row)
    shares = ("y", "zh", "core")
    out_specs = (row, row, P(shares, None), P(shares))
    return jax.shard_map(local, mesh=wide, in_specs=in_specs, out_specs=out_specs, check_vma=False)
```

```python
import math

import jax
import jax.numpy as jnp
from jax import lax
from jax.experimental import pallas as pl
from jax.experimental.pallas import tpu as pltpu
from jax.sharding import Mesh
from jax.sharding import PartitionSpec as P

AXES = ("y", "zh", "core", "x", "zl")
SIZES = (8, 2, 2, 4, 6)
NODE = AXES
BITS = 5
VMEM_LIMIT = 20 * 2**20
f32 = jnp.float32
bf16 = jnp.bfloat16


def permute(array, axes, route):
    peers = lax.axis_size(axes)
    return lax.ppermute(array, axes, [(i, route(i) % peers) for i in range(peers)])


def near_partner(i):
    return i ^ 1


def far_partner(i):
    return i + 1 if i % 2 else i - 1


def rows_dot(a, b):
    return jnp.dot(a, b, preferred_element_type=f32)


def transposed_dot(a, b):
    return lax.dot_general(a, b, (((0,), (0,)), ((), ())), preferred_element_type=f32)


def adjacency_kernel(slot_ref, nbr_ref, cnt_ref, adj_ref, edge_ref, own_ref):
    tile = pl.program_id(0)
    rows, width = nbr_ref.shape
    slots = slot_ref.shape[1]
    tiles = adj_ref.shape[1] // rows
    own_first = tiles // 3
    nbr = nbr_ref[...]
    live = lax.broadcasted_iota(jnp.int32, nbr.shape, 1) < cnt_ref[...]
    low = jnp.bitwise_and(nbr, rows - 1)
    shift = BITS * lax.shift_right_logical(nbr, rows.bit_length() - 1)
    step = jnp.where(live, lax.shift_left(jnp.ones_like(nbr), shift), 0)
    lane = lax.broadcasted_iota(jnp.int32, (rows, rows), 1)
    packed = jnp.zeros((rows, rows), jnp.int32)
    for k in range(width):
        packed += jnp.where(lane == low[:, k : k + 1], step[:, k : k + 1], 0)
    adj_ref[...] = jnp.zeros_like(adj_ref)
    row = lax.broadcasted_iota(jnp.int32, (rows, rows), 0)
    own = pl.ds(pl.multiple_of((own_first + tile) * rows, rows), rows)
    adj_ref[:, own] = (row == lane).astype(f32).astype(bf16)
    for s in range(slots):
        counts = jnp.bitwise_and(lax.shift_right_logical(packed, BITS * s), 2**BITS - 1)
        place = pl.ds(pl.multiple_of(slot_ref[tile, s] * rows, rows), rows)
        adj_ref[:, place] += counts.astype(f32).astype(bf16)
    nodes = tiles // 3 * rows
    edge_ref[0:nodes, :] = adj_ref[:, 0:nodes].T
    edge_ref[nodes : 2 * nodes, :] = adj_ref[:, 2 * nodes : 3 * nodes].T
    own_ref[...] = adj_ref[:, nodes : 2 * nodes].T


def build_adjacency(local_slot, neighbours, counts):
    tiles, slots = local_slot.shape
    nodes, width = neighbours.shape
    rows = nodes // tiles
    window = 3 * nodes
    return pl.pallas_call(
        adjacency_kernel,
        grid=(tiles,),
        in_specs=[
            pl.BlockSpec(memory_space=pltpu.SMEM),
            pl.BlockSpec((rows, width), lambda t: (t, 0)),
            pl.BlockSpec((rows, 1), lambda t: (t, 0)),
        ],
        out_specs=[
            pl.BlockSpec((rows, window), lambda t: (t, 0)),
            pl.BlockSpec((2 * nodes, rows), lambda t: (0, t)),
            pl.BlockSpec((nodes, rows), lambda t: (0, t)),
        ],
        out_shape=[
            jax.ShapeDtypeStruct((nodes, window), bf16),
            jax.ShapeDtypeStruct((2 * nodes, nodes), bf16),
            jax.ShapeDtypeStruct((nodes, nodes), bf16),
        ],
        cost_estimate=pl.CostEstimate(flops=10**9, bytes_accessed=8 * 10**6, transcendentals=0),
        compiler_params=pltpu.CompilerParams(vmem_limit_bytes=VMEM_LIMIT),
        name="adjacency",
    )(local_slot, neighbours, counts)


def forward_kernel(
    core_ref, adj, edge, own, near, far, weight, bias, root, grad,
    hidden, wsend, wkeep, scaled, part_near, part_far, agg_s, pre_s,
):
    nodes, width = own.shape
    rows = 128
    for first in range(0, nodes, rows):
        r = pl.ds(first, rows)
        agg = rows_dot(adj[r, 0:nodes], near[...])
        agg += rows_dot(adj[r, nodes : 2 * nodes], own[...])
        agg += rows_dot(adj[r, 2 * nodes : 3 * nodes], far[...])
        agg = agg.astype(bf16)
        agg_s[r, :] = agg
        pre = root[r, :] * rows_dot(agg, weight[...]) + bias[...]
        gate = jax.nn.sigmoid(pre)
        hidden[r, :] = (pre * gate).astype(bf16)
        grad_pre = grad[r, :].astype(f32) * gate * (1.0 + pre * (1.0 - gate))
        pre_s[r, :] = grad_pre.astype(bf16)
        scaled[r, :] = (grad_pre * root[r, :]).astype(bf16)
    core = core_ref[0]
    ones = jnp.ones((nodes, 128), bf16)
    wgrad = transposed_dot(agg_s[...], scaled[...]).astype(bf16)
    bgrad = transposed_dot(pre_s[...], ones).astype(bf16)
    share = 16
    for chunk in range(width // share):
        outer, side = divmod(chunk, 2)
        band = slice(chunk * share, (chunk + 1) * share)
        place = pl.ds(outer * share, share)

        @pl.when(core == side)
        def _():
            wkeep[place, 0:width] = wgrad[band]
            wkeep[place, width : width + 128] = bgrad[band]

        @pl.when(core != side)
        def _():
            wsend[place, 0:width] = wgrad[band]
            wsend[place, width : width + 128] = bgrad[band]
    for first in range(0, nodes, rows):
        part = rows_dot(edge[first : first + rows, :], scaled[...])
        part_near[first : first + rows, :] = part.astype(bf16)
        part = rows_dot(edge[nodes + first : nodes + first + rows, :], scaled[...])
        part_far[first : first + rows, :] = part.astype(bf16)


def forward(core, adj, edge, own, near, far, weight, bias, root, grad):
    nodes, width = own.shape
    half = jax.ShapeDtypeStruct((width // 2, width + 128), bf16)
    square = jax.ShapeDtypeStruct((nodes, width), bf16)
    vmem = pl.BlockSpec(memory_space=pltpu.VMEM)
    return pl.pallas_call(
        forward_kernel,
        in_specs=[pl.BlockSpec(memory_space=pltpu.SMEM)] + [vmem] * 9,
        out_specs=[vmem] * 6,
        out_shape=[square, half, half, square, square, square],
        scratch_shapes=[pltpu.VMEM((nodes, width), bf16)] * 2,
        compiler_params=pltpu.CompilerParams(vmem_limit_bytes=VMEM_LIMIT),
        cost_estimate=pl.CostEstimate(flops=10**9, bytes_accessed=10**7, transcendentals=0),
        name="forward",
    )(core, adj, edge, own, near, far, weight, bias, root, grad)


def spread_kernel(blocks, out):
    count = blocks.shape[0]
    total = blocks[0].astype(f32)
    for i in range(1, count):
        total += blocks[i].astype(f32)
    total = total.astype(bf16)
    copies, rows = out.shape[0], out.shape[1]
    each = copies * rows // blocks.shape[1]
    for i in range(copies):
        first = i // each * rows
        out[i] = total[first : first + rows]


def spread(blocks, pieces, copies):
    _, rows, width = blocks.shape
    vmem = pl.BlockSpec(memory_space=pltpu.VMEM)
    return pl.pallas_call(
        spread_kernel,
        in_specs=[vmem],
        out_specs=vmem,
        out_shape=jax.ShapeDtypeStruct((pieces * copies, rows // pieces, width), bf16),
        compiler_params=pltpu.CompilerParams(vmem_limit_bytes=VMEM_LIMIT),
        cost_estimate=pl.CostEstimate(flops=10**6, bytes_accessed=10**6, transcendentals=0),
        name="spread",
    )(blocks)


def halves_kernel(high_ref, blocks, sent, kept):
    count = blocks.shape[0]
    rows = sent.shape[0]
    for half, out_type in ((1 - high_ref[0], "sent"), (high_ref[0], "kept")):
        r = pl.ds(pl.multiple_of(half * rows, rows), rows)
        total = blocks[0, r, :].astype(f32)
        for i in range(1, count):
            total += blocks[i, r, :].astype(f32)
        if out_type == "sent":
            sent[...] = total.astype(bf16)
        else:
            kept[...] = total


def halves(high, blocks):
    _, rows, width = blocks.shape
    vmem = pl.BlockSpec(memory_space=pltpu.VMEM)
    return pl.pallas_call(
        halves_kernel,
        in_specs=[pl.BlockSpec(memory_space=pltpu.SMEM), vmem],
        out_specs=[vmem] * 2,
        out_shape=[
            jax.ShapeDtypeStruct((rows // 2, width), bf16),
            jax.ShapeDtypeStruct((rows // 2, width), f32),
        ],
        compiler_params=pltpu.CompilerParams(vmem_limit_bytes=VMEM_LIMIT),
        cost_estimate=pl.CostEstimate(flops=10**6, bytes_accessed=10**6, transcendentals=0),
        name="halves",
    )(high, blocks)


def merge_kernel(kept, pair, out):
    total = (kept[...] + pair[...].astype(f32)).astype(bf16)
    for i in range(out.shape[0]):
        out[i] = total


def merge(kept, pair, copies):
    vmem = pl.BlockSpec(memory_space=pltpu.VMEM)
    return pl.pallas_call(
        merge_kernel,
        in_specs=[vmem] * 2,
        out_specs=vmem,
        out_shape=jax.ShapeDtypeStruct((copies, *kept.shape), bf16),
        compiler_params=pltpu.CompilerParams(vmem_limit_bytes=VMEM_LIMIT),
        cost_estimate=pl.CostEstimate(flops=10**6, bytes_accessed=10**6, transcendentals=0),
        name="merge",
    )(kept, pair)


def last_sum_kernel(scale, blocks, out, bias):
    count, rows, width = blocks.shape
    total = blocks[0].astype(f32)
    for i in range(1, count):
        total += blocks[i].astype(f32)
    total = total * scale
    wide = out.shape[1]
    out[...] = total[:, 0:wide]
    column = total[:, wide:width]
    row = lax.broadcasted_iota(jnp.int32, column.shape, 0)
    lane = lax.broadcasted_iota(jnp.int32, column.shape, 1)
    flat = jnp.sum(jnp.where(row == lane, column, 0.0), axis=0, keepdims=True)
    bias[...] = flat[:, 0:rows]


def last_sum(blocks, scale):
    _, rows, width = blocks.shape
    vmem = pl.BlockSpec(memory_space=pltpu.VMEM)
    return pl.pallas_call(
        lambda *refs: last_sum_kernel(scale, *refs),
        in_specs=[vmem],
        out_specs=[vmem] * 2,
        out_shape=[
            jax.ShapeDtypeStruct((rows, width - 128), f32),
            jax.ShapeDtypeStruct((1, rows), f32),
        ],
        compiler_params=pltpu.CompilerParams(vmem_limit_bytes=VMEM_LIMIT),
        cost_estimate=pl.CostEstimate(flops=10**6, bytes_accessed=10**6, transcendentals=0),
        name="last_sum",
    )(blocks)


def own_part_kernel(adj, scaled, out):
    rows = 128
    for first in range(0, out.shape[0], rows):
        out[first : first + rows, :] = rows_dot(adj[first : first + rows, :], scaled[...])


def own_part(adj, scaled):
    vmem = pl.BlockSpec(memory_space=pltpu.VMEM)
    return pl.pallas_call(
        own_part_kernel,
        in_specs=[vmem] * 2,
        out_specs=vmem,
        out_shape=jax.ShapeDtypeStruct(scaled.shape, f32),
        compiler_params=pltpu.CompilerParams(vmem_limit_bytes=VMEM_LIMIT),
        cost_estimate=pl.CostEstimate(flops=10**12, bytes_accessed=10**9, transcendentals=0),
        name="own_part",
    )(adj, scaled)


def final_kernel(part_own, from_near, from_far, root, weight, out):
    nodes = out.shape[0]
    rows = 128
    for first in range(0, nodes, rows):
        r = pl.ds(first, rows)
        total = part_own[r, :] + from_near[r, :].astype(f32) + from_far[r, :].astype(f32)
        grad_proj = (root[r, :] * total).astype(bf16)
        out[r, :] = lax.dot_general(
            grad_proj, weight[...], (((1,), (1,)), ((), ())), preferred_element_type=f32
        ).astype(bf16)


def final(part_own, from_near, from_far, root, weight):
    vmem = pl.BlockSpec(memory_space=pltpu.VMEM)
    return pl.pallas_call(
        final_kernel,
        in_specs=[vmem] * 5,
        out_specs=vmem,
        out_shape=jax.ShapeDtypeStruct(part_own.shape, bf16),
        cost_estimate=pl.CostEstimate(flops=10**8, bytes_accessed=10**6, transcendentals=0),
        compiler_params=pltpu.CompilerParams(vmem_limit_bytes=VMEM_LIMIT),
        name="final",
    )(part_own, from_near, from_far, root, weight)


def local(features, weight, layer_bias, block_cols, neighbours, row_counts, out_grad):
    nodes, width = features.shape
    tile_count = block_cols.shape[0]
    devices = lax.axis_size(NODE)
    all_tiles = tile_count * devices
    normaliser = 1.0 / math.sqrt(nodes * devices)
    window_start = (lax.axis_index(NODE) - 1) * tile_count
    local_slot = jnp.mod(block_cols - window_start, all_tiles)
    group = local_slot // tile_count
    even = lax.axis_index(NODE) % 2 == 0
    local_slot = jnp.where(even, local_slot + 2 * (1 - group) * tile_count, local_slot)
    counts = row_counts[:, None]
    root = lax.rsqrt(1.0 + counts.astype(f32))
    own = (features.astype(f32) * root).astype(bf16)
    far = permute(own, NODE, far_partner)
    near = permute(own, NODE, near_partner)
    adj, edge, own_t = build_adjacency(local_slot, neighbours, counts)
    core = lax.axis_index("core").astype(jnp.int32).reshape(1)
    hidden, wsend, wkeep, scaled, part_near, part_far = forward(
        core, adj, edge, own, near, far, weight, layer_bias[None, :], root, out_grad
    )
    got = permute(wsend, "core", lambda i: i ^ 1)
    from_near = permute(part_near, NODE, near_partner)
    ny, nx, nzl = (lax.axis_size(n) for n in ("y", "x", "zl"))
    chip = (wkeep.astype(f32) + got.astype(f32)).astype(bf16)
    part_far, chip = lax.optimization_barrier((part_far, chip))
    from_far = permute(part_far, NODE, far_partner)
    blocks = lax.all_to_all(chip.reshape(ny, -1, width + 128), "y", 0, 0)
    own_t, from_near = lax.optimization_barrier((own_t, from_near))
    part_own = own_part(own_t, scaled)
    blocks, part_own = lax.optimization_barrier((blocks, part_own))
    blocks = lax.all_to_all(spread(blocks, 1, nx), "x", 0, 0)
    high = lax.axis_index("zh").astype(jnp.int32).reshape(1)
    sent, kept = halves(high, blocks)
    pair = permute(sent, ("zh", "zl"), lambda i: -1 - i)
    blocks = merge(kept, pair, nzl)
    blocks, from_far = lax.optimization_barrier((blocks, from_far))
    blocks = lax.all_to_all(blocks, "zl", 0, 0)
    weight_grad, bias_grad = last_sum(blocks, normaliser)
    input_grad = final(part_own, from_near, from_far, root, weight)
    return (hidden, input_grad, weight_grad, bias_grad[0])


def solution(mesh):
    wide = Mesh(mesh.devices.reshape(SIZES), AXES)
    row = P(NODE, None)
    in_specs = (row, P(), P(), row, row, P(NODE), row)
    shares = ("y", "zh", "core")
    out_specs = (row, row, P(shares, None), P(shares))
    return jax.shard_map(local, mesh=wide, in_specs=in_specs, out_specs=out_specs, check_vma=False)
```

```python
import math

import jax
import jax.numpy as jnp
from jax import lax
from jax.experimental import pallas as pl
from jax.experimental.pallas import tpu as pltpu
from jax.sharding import Mesh
from jax.sharding import PartitionSpec as P

AXES = ("y", "zh", "core", "x", "zl")
SIZES = (8, 2, 2, 4, 6)
NODE = AXES
BITS = 5
VMEM_LIMIT = 20 * 2**20
f32 = jnp.float32
bf16 = jnp.bfloat16


def permute(array, axes, route):
    peers = lax.axis_size(axes)
    return lax.ppermute(array, axes, [(i, route(i) % peers) for i in range(peers)])


def near_partner(i):
    return i ^ 1


def far_partner(i):
    return i + 1 if i % 2 else i - 1


def rows_dot(a, b):
    return jnp.dot(a, b, preferred_element_type=f32)


def transposed_dot(a, b):
    return lax.dot_general(a, b, (((0,), (0,)), ((), ())), preferred_element_type=f32)


def adjacency_kernel(slot_ref, nbr_ref, cnt_ref, adj_ref, edge_ref, own_ref):
    tile = pl.program_id(0)
    rows, width = nbr_ref.shape
    slots = slot_ref.shape[1]
    tiles = adj_ref.shape[1] // rows
    own_first = tiles // 3
    nbr = nbr_ref[...]
    live = lax.broadcasted_iota(jnp.int32, nbr.shape, 1) < cnt_ref[...]
    low = jnp.bitwise_and(nbr, rows - 1)
    shift = BITS * lax.shift_right_logical(nbr, rows.bit_length() - 1)
    step = jnp.where(live, lax.shift_left(jnp.ones_like(nbr), shift), 0)
    lane = lax.broadcasted_iota(jnp.int32, (rows, rows), 1)
    packed = jnp.zeros((rows, rows), jnp.int32)
    for k in range(width):
        packed += jnp.where(lane == low[:, k : k + 1], step[:, k : k + 1], 0)
    adj_ref[...] = jnp.zeros_like(adj_ref)
    row = lax.broadcasted_iota(jnp.int32, (rows, rows), 0)
    own = pl.ds(pl.multiple_of((own_first + tile) * rows, rows), rows)
    adj_ref[:, own] = (row == lane).astype(f32).astype(bf16)
    for s in range(slots):
        counts = jnp.bitwise_and(lax.shift_right_logical(packed, BITS * s), 2**BITS - 1)
        place = pl.ds(pl.multiple_of(slot_ref[tile, s] * rows, rows), rows)
        adj_ref[:, place] += counts.astype(f32).astype(bf16)
    nodes = tiles // 3 * rows
    edge_ref[0:nodes, :] = adj_ref[:, 0:nodes].T
    edge_ref[nodes : 2 * nodes, :] = adj_ref[:, 2 * nodes : 3 * nodes].T
    own_ref[...] = adj_ref[:, nodes : 2 * nodes].T


def build_adjacency(local_slot, neighbours, counts):
    tiles, slots = local_slot.shape
    nodes, width = neighbours.shape
    rows = nodes // tiles
    window = 3 * nodes
    return pl.pallas_call(
        adjacency_kernel,
        grid=(tiles,),
        in_specs=[
            pl.BlockSpec(memory_space=pltpu.SMEM),
            pl.BlockSpec((rows, width), lambda t: (t, 0)),
            pl.BlockSpec((rows, 1), lambda t: (t, 0)),
        ],
        out_specs=[
            pl.BlockSpec((rows, window), lambda t: (t, 0)),
            pl.BlockSpec((2 * nodes, rows), lambda t: (0, t)),
            pl.BlockSpec((nodes, rows), lambda t: (0, t)),
        ],
        out_shape=[
            jax.ShapeDtypeStruct((nodes, window), bf16),
            jax.ShapeDtypeStruct((2 * nodes, nodes), bf16),
            jax.ShapeDtypeStruct((nodes, nodes), bf16),
        ],
        cost_estimate=pl.CostEstimate(flops=10**9, bytes_accessed=8 * 10**6, transcendentals=0),
        compiler_params=pltpu.CompilerParams(vmem_limit_bytes=VMEM_LIMIT),
        name="adjacency",
    )(local_slot, neighbours, counts)


def forward_kernel(
    core_ref, adj, own, near, far, weight, bias, root, grad,
    hidden, wsend, wkeep, scaled, agg_s, pre_s,
):
    nodes, width = own.shape
    rows = 128
    for first in range(0, nodes, rows):
        r = pl.ds(first, rows)
        agg = rows_dot(adj[r, 0:nodes], near[...])
        agg += rows_dot(adj[r, nodes : 2 * nodes], own[...])
        agg += rows_dot(adj[r, 2 * nodes : 3 * nodes], far[...])
        agg = agg.astype(bf16)
        agg_s[r, :] = agg
        pre = root[r, :] * rows_dot(agg, weight[...]) + bias[...]
        gate = jax.nn.sigmoid(pre)
        hidden[r, :] = (pre * gate).astype(bf16)
        grad_pre = grad[r, :].astype(f32) * gate * (1.0 + pre * (1.0 - gate))
        pre_s[r, :] = grad_pre.astype(bf16)
        scaled[r, :] = (grad_pre * root[r, :]).astype(bf16)
    core = core_ref[0]
    ones = jnp.ones((nodes, 128), bf16)
    wgrad = transposed_dot(agg_s[...], scaled[...]).astype(bf16)
    bgrad = transposed_dot(pre_s[...], ones).astype(bf16)
    share = 16
    for chunk in range(width // share):
        outer, side = divmod(chunk, 2)
        band = slice(chunk * share, (chunk + 1) * share)
        place = pl.ds(outer * share, share)

        @pl.when(core == side)
        def _():
            wkeep[place, 0:width] = wgrad[band]
            wkeep[place, width : width + 128] = bgrad[band]

        @pl.when(core != side)
        def _():
            wsend[place, 0:width] = wgrad[band]
            wsend[place, width : width + 128] = bgrad[band]


def forward(core, adj, own, near, far, weight, bias, root, grad):
    nodes, width = own.shape
    half = jax.ShapeDtypeStruct((width // 2, width + 128), bf16)
    square = jax.ShapeDtypeStruct((nodes, width), bf16)
    vmem = pl.BlockSpec(memory_space=pltpu.VMEM)
    return pl.pallas_call(
        forward_kernel,
        in_specs=[pl.BlockSpec(memory_space=pltpu.SMEM)] + [vmem] * 8,
        out_specs=[vmem] * 4,
        out_shape=[square, half, half, square],
        scratch_shapes=[pltpu.VMEM((nodes, width), bf16)] * 2,
        compiler_params=pltpu.CompilerParams(vmem_limit_bytes=VMEM_LIMIT),
        cost_estimate=pl.CostEstimate(flops=10**9, bytes_accessed=10**7, transcendentals=0),
        name="forward",
    )(core, adj, own, near, far, weight, bias, root, grad)


def parts_kernel(edge, scaled, part_near, part_far):
    nodes = scaled.shape[0]
    rows = 128
    for first in range(0, nodes, rows):
        part = rows_dot(edge[first : first + rows, :], scaled[...])
        part_near[first : first + rows, :] = part.astype(bf16)
        part = rows_dot(edge[nodes + first : nodes + first + rows, :], scaled[...])
        part_far[first : first + rows, :] = part.astype(bf16)


def parts(edge, scaled):
    square = jax.ShapeDtypeStruct(scaled.shape, bf16)
    vmem = pl.BlockSpec(memory_space=pltpu.VMEM)
    return pl.pallas_call(
        parts_kernel,
        in_specs=[vmem] * 2,
        out_specs=[vmem] * 2,
        out_shape=[square, square],
        compiler_params=pltpu.CompilerParams(vmem_limit_bytes=VMEM_LIMIT),
        cost_estimate=pl.CostEstimate(flops=10**8, bytes_accessed=10**6, transcendentals=0),
        name="parts",
    )(edge, scaled)


def spread_kernel(blocks, out):
    count = blocks.shape[0]
    total = blocks[0].astype(f32)
    for i in range(1, count):
        total += blocks[i].astype(f32)
    total = total.astype(bf16)
    copies, rows = out.shape[0], out.shape[1]
    each = copies * rows // blocks.shape[1]
    for i in range(copies):
        first = i // each * rows
        out[i] = total[first : first + rows]


def spread(blocks, pieces, copies):
    _, rows, width = blocks.shape
    vmem = pl.BlockSpec(memory_space=pltpu.VMEM)
    return pl.pallas_call(
        spread_kernel,
        in_specs=[vmem],
        out_specs=vmem,
        out_shape=jax.ShapeDtypeStruct((pieces * copies, rows // pieces, width), bf16),
        compiler_params=pltpu.CompilerParams(vmem_limit_bytes=VMEM_LIMIT),
        cost_estimate=pl.CostEstimate(flops=10**6, bytes_accessed=10**6, transcendentals=0),
        name="spread",
    )(blocks)


def halves_kernel(high_ref, blocks, sent, kept):
    count = blocks.shape[0]
    rows = sent.shape[0]
    for half, out_type in ((1 - high_ref[0], "sent"), (high_ref[0], "kept")):
        r = pl.ds(pl.multiple_of(half * rows, rows), rows)
        total = blocks[0, r, :].astype(f32)
        for i in range(1, count):
            total += blocks[i, r, :].astype(f32)
        if out_type == "sent":
            sent[...] = total.astype(bf16)
        else:
            kept[...] = total


def halves(high, blocks):
    _, rows, width = blocks.shape
    vmem = pl.BlockSpec(memory_space=pltpu.VMEM)
    return pl.pallas_call(
        halves_kernel,
        in_specs=[pl.BlockSpec(memory_space=pltpu.SMEM), vmem],
        out_specs=[vmem] * 2,
        out_shape=[
            jax.ShapeDtypeStruct((rows // 2, width), bf16),
            jax.ShapeDtypeStruct((rows // 2, width), f32),
        ],
        compiler_params=pltpu.CompilerParams(vmem_limit_bytes=VMEM_LIMIT),
        cost_estimate=pl.CostEstimate(flops=10**6, bytes_accessed=10**6, transcendentals=0),
        name="halves",
    )(high, blocks)


def merge_kernel(kept, pair, out):
    total = (kept[...] + pair[...].astype(f32)).astype(bf16)
    for i in range(out.shape[0]):
        out[i] = total


def merge(kept, pair, copies):
    vmem = pl.BlockSpec(memory_space=pltpu.VMEM)
    return pl.pallas_call(
        merge_kernel,
        in_specs=[vmem] * 2,
        out_specs=vmem,
        out_shape=jax.ShapeDtypeStruct((copies, *kept.shape), bf16),
        compiler_params=pltpu.CompilerParams(vmem_limit_bytes=VMEM_LIMIT),
        cost_estimate=pl.CostEstimate(flops=10**6, bytes_accessed=10**6, transcendentals=0),
        name="merge",
    )(kept, pair)


def last_sum_kernel(scale, blocks, out, bias):
    count, rows, width = blocks.shape
    total = blocks[0].astype(f32)
    for i in range(1, count):
        total += blocks[i].astype(f32)
    total = total * scale
    wide = out.shape[1]
    out[...] = total[:, 0:wide]
    column = total[:, wide:width]
    row = lax.broadcasted_iota(jnp.int32, column.shape, 0)
    lane = lax.broadcasted_iota(jnp.int32, column.shape, 1)
    flat = jnp.sum(jnp.where(row == lane, column, 0.0), axis=0, keepdims=True)
    bias[...] = flat[:, 0:rows]


def last_sum(blocks, scale):
    _, rows, width = blocks.shape
    vmem = pl.BlockSpec(memory_space=pltpu.VMEM)
    return pl.pallas_call(
        lambda *refs: last_sum_kernel(scale, *refs),
        in_specs=[vmem],
        out_specs=[vmem] * 2,
        out_shape=[
            jax.ShapeDtypeStruct((rows, width - 128), f32),
            jax.ShapeDtypeStruct((1, rows), f32),
        ],
        compiler_params=pltpu.CompilerParams(vmem_limit_bytes=VMEM_LIMIT),
        cost_estimate=pl.CostEstimate(flops=10**6, bytes_accessed=10**6, transcendentals=0),
        name="last_sum",
    )(blocks)


def own_part_kernel(adj, scaled, out):
    rows = 128
    for first in range(0, out.shape[0], rows):
        out[first : first + rows, :] = rows_dot(adj[first : first + rows, :], scaled[...])


def own_part(adj, scaled):
    vmem = pl.BlockSpec(memory_space=pltpu.VMEM)
    return pl.pallas_call(
        own_part_kernel,
        in_specs=[vmem] * 2,
        out_specs=vmem,
        out_shape=jax.ShapeDtypeStruct(scaled.shape, f32),
        compiler_params=pltpu.CompilerParams(vmem_limit_bytes=VMEM_LIMIT),
        cost_estimate=pl.CostEstimate(flops=10**8, bytes_accessed=10**6, transcendentals=0),
        name="own_part",
    )(adj, scaled)


def final_kernel(part_own, from_near, from_far, root, weight, out):
    nodes = out.shape[0]
    rows = 128
    for first in range(0, nodes, rows):
        r = pl.ds(first, rows)
        total = part_own[r, :] + from_near[r, :].astype(f32) + from_far[r, :].astype(f32)
        grad_proj = (root[r, :] * total).astype(bf16)
        out[r, :] = lax.dot_general(
            grad_proj, weight[...], (((1,), (1,)), ((), ())), preferred_element_type=f32
        ).astype(bf16)


def final(part_own, from_near, from_far, root, weight):
    vmem = pl.BlockSpec(memory_space=pltpu.VMEM)
    return pl.pallas_call(
        final_kernel,
        in_specs=[vmem] * 5,
        out_specs=vmem,
        out_shape=jax.ShapeDtypeStruct(part_own.shape, bf16),
        cost_estimate=pl.CostEstimate(flops=10**8, bytes_accessed=10**6, transcendentals=0),
        compiler_params=pltpu.CompilerParams(vmem_limit_bytes=VMEM_LIMIT),
        name="final",
    )(part_own, from_near, from_far, root, weight)


def local(features, weight, layer_bias, block_cols, neighbours, row_counts, out_grad):
    nodes, width = features.shape
    tile_count = block_cols.shape[0]
    devices = lax.axis_size(NODE)
    all_tiles = tile_count * devices
    normaliser = 1.0 / math.sqrt(nodes * devices)
    window_start = (lax.axis_index(NODE) - 1) * tile_count
    local_slot = jnp.mod(block_cols - window_start, all_tiles)
    group = local_slot // tile_count
    even = lax.axis_index(NODE) % 2 == 0
    local_slot = jnp.where(even, local_slot + 2 * (1 - group) * tile_count, local_slot)
    counts = row_counts[:, None]
    root = lax.rsqrt(1.0 + counts.astype(f32))
    own = (features.astype(f32) * root).astype(bf16)
    far = permute(own, NODE, far_partner)
    near = permute(own, NODE, near_partner)
    adj, edge, own_t = build_adjacency(local_slot, neighbours, counts)
    core = lax.axis_index("core").astype(jnp.int32).reshape(1)
    hidden, wsend, wkeep, scaled = forward(
        core, adj, own, near, far, weight, layer_bias[None, :], root, out_grad
    )
    got = permute(wsend, "core", lambda i: i ^ 1)
    ny, nx, nzl = (lax.axis_size(n) for n in ("y", "x", "zl"))
    chip = (wkeep.astype(f32) + got.astype(f32)).astype(bf16)
    scaled, chip = lax.optimization_barrier((scaled, chip))
    part_near, part_far = parts(edge, scaled)
    from_near = permute(part_near, NODE, near_partner)
    from_far = permute(part_far, NODE, far_partner)
    blocks = lax.all_to_all(chip.reshape(ny, -1, width + 128), "y", 0, 0)
    part_own = own_part(own_t, scaled)
    blocks = lax.all_to_all(spread(blocks, 1, nx), "x", 0, 0)
    high = lax.axis_index("zh").astype(jnp.int32).reshape(1)
    sent, kept = halves(high, blocks)
    pair = permute(sent, ("zh", "zl"), lambda i: -1 - i)
    blocks = merge(kept, pair, nzl)
    blocks, from_near, from_far = lax.optimization_barrier((blocks, from_near, from_far))
    blocks = lax.all_to_all(blocks, "zl", 0, 0)
    weight_grad, bias_grad = last_sum(blocks, normaliser)
    input_grad = final(part_own, from_near, from_far, root, weight)
    return (hidden, input_grad, weight_grad, bias_grad[0])


def solution(mesh):
    wide = Mesh(mesh.devices.reshape(SIZES), AXES)
    row = P(NODE, None)
    in_specs = (row, P(), P(), row, row, P(NODE), row)
    shares = ("y", "zh", "core")
    out_specs = (row, row, P(shares, None), P(shares))
    return jax.shard_map(local, mesh=wide, in_specs=in_specs, out_specs=out_specs, check_vma=False)
```

```python
import math

import jax
import jax.numpy as jnp
from jax import lax
from jax.experimental import pallas as pl
from jax.experimental.pallas import tpu as pltpu
from jax.sharding import Mesh
from jax.sharding import PartitionSpec as P

AXES = ("y", "zh", "core", "x", "zl")
SIZES = (8, 2, 2, 4, 6)
NODE = AXES
BITS = 5
VMEM_LIMIT = 20 * 2**20
f32 = jnp.float32
bf16 = jnp.bfloat16


def permute(array, axes, route):
    peers = lax.axis_size(axes)
    return lax.ppermute(array, axes, [(i, route(i) % peers) for i in range(peers)])


def near_partner(i):
    return i ^ 1


def far_partner(i):
    return i + 1 if i % 2 else i - 1


def rows_dot(a, b):
    return jnp.dot(a, b, preferred_element_type=f32)


def transposed_dot(a, b):
    return lax.dot_general(a, b, (((0,), (0,)), ((), ())), preferred_element_type=f32)


def adjacency_kernel(slot_ref, nbr_ref, cnt_ref, adj_ref, edge_ref, own_ref):
    tile = pl.program_id(0)
    rows, width = nbr_ref.shape
    slots = slot_ref.shape[1]
    tiles = adj_ref.shape[1] // rows
    own_first = tiles // 3
    nbr = nbr_ref[...]
    live = lax.broadcasted_iota(jnp.int32, nbr.shape, 1) < cnt_ref[...]
    low = jnp.bitwise_and(nbr, rows - 1)
    shift = BITS * lax.shift_right_logical(nbr, rows.bit_length() - 1)
    step = jnp.where(live, lax.shift_left(jnp.ones_like(nbr), shift), 0)
    lane = lax.broadcasted_iota(jnp.int32, (rows, rows), 1)
    packed = jnp.zeros((rows, rows), jnp.int32)
    for k in range(width):
        packed += jnp.where(lane == low[:, k : k + 1], step[:, k : k + 1], 0)
    adj_ref[...] = jnp.zeros_like(adj_ref)
    row = lax.broadcasted_iota(jnp.int32, (rows, rows), 0)
    own = pl.ds(pl.multiple_of((own_first + tile) * rows, rows), rows)
    adj_ref[:, own] = (row == lane).astype(f32).astype(bf16)
    for s in range(slots):
        counts = jnp.bitwise_and(lax.shift_right_logical(packed, BITS * s), 2**BITS - 1)
        place = pl.ds(pl.multiple_of(slot_ref[tile, s] * rows, rows), rows)
        adj_ref[:, place] += counts.astype(f32).astype(bf16)
    nodes = tiles // 3 * rows
    edge_ref[0:nodes, :] = adj_ref[:, 0:nodes].T
    edge_ref[nodes : 2 * nodes, :] = adj_ref[:, 2 * nodes : 3 * nodes].T
    own_ref[...] = adj_ref[:, nodes : 2 * nodes].T


def build_adjacency(local_slot, neighbours, counts):
    tiles, slots = local_slot.shape
    nodes, width = neighbours.shape
    rows = nodes // tiles
    window = 3 * nodes
    return pl.pallas_call(
        adjacency_kernel,
        grid=(tiles,),
        in_specs=[
            pl.BlockSpec(memory_space=pltpu.SMEM),
            pl.BlockSpec((rows, width), lambda t: (t, 0)),
            pl.BlockSpec((rows, 1), lambda t: (t, 0)),
        ],
        out_specs=[
            pl.BlockSpec((rows, window), lambda t: (t, 0)),
            pl.BlockSpec((2 * nodes, rows), lambda t: (0, t)),
            pl.BlockSpec((nodes, rows), lambda t: (0, t)),
        ],
        out_shape=[
            jax.ShapeDtypeStruct((nodes, window), bf16),
            jax.ShapeDtypeStruct((2 * nodes, nodes), bf16),
            jax.ShapeDtypeStruct((nodes, nodes), bf16),
        ],
        cost_estimate=pl.CostEstimate(flops=10**9, bytes_accessed=8 * 10**6, transcendentals=0),
        compiler_params=pltpu.CompilerParams(vmem_limit_bytes=VMEM_LIMIT),
        name="adjacency",
    )(local_slot, neighbours, counts)


def forward_kernel(
    core_ref, adj, edge, own, near, far, weight, bias, root, grad,
    hidden, wsend, wkeep, scaled, part_near, part_far, agg_s, pre_s,
):
    nodes, width = own.shape
    rows = 128
    for first in range(0, nodes, rows):
        r = pl.ds(first, rows)
        agg = rows_dot(adj[r, 0:nodes], near[...])
        agg += rows_dot(adj[r, nodes : 2 * nodes], own[...])
        agg += rows_dot(adj[r, 2 * nodes : 3 * nodes], far[...])
        agg = agg.astype(bf16)
        agg_s[r, :] = agg
        pre = root[r, :] * rows_dot(agg, weight[...]) + bias[...]
        gate = jax.nn.sigmoid(pre)
        hidden[r, :] = (pre * gate).astype(bf16)
        grad_pre = grad[r, :].astype(f32) * gate * (1.0 + pre * (1.0 - gate))
        pre_s[r, :] = grad_pre.astype(bf16)
        scaled[r, :] = (grad_pre * root[r, :]).astype(bf16)
    core = core_ref[0]
    ones = jnp.ones((nodes, 128), bf16)
    wgrad = transposed_dot(agg_s[...], scaled[...]).astype(bf16)
    bgrad = transposed_dot(pre_s[...], ones).astype(bf16)
    share = 16
    for chunk in range(width // share):
        outer, side = divmod(chunk, 2)
        band = slice(chunk * share, (chunk + 1) * share)
        place = pl.ds(outer * share, share)

        @pl.when(core == side)
        def _():
            wkeep[place, 0:width] = wgrad[band]
            wkeep[place, width : width + 128] = bgrad[band]

        @pl.when(core != side)
        def _():
            wsend[place, 0:width] = wgrad[band]
            wsend[place, width : width + 128] = bgrad[band]
    for first in range(0, nodes, rows):
        part = rows_dot(edge[first : first + rows, :], scaled[...])
        part_near[first : first + rows, :] = part.astype(bf16)
        part = rows_dot(edge[nodes + first : nodes + first + rows, :], scaled[...])
        part_far[first : first + rows, :] = part.astype(bf16)


def forward(core, adj, edge, own, near, far, weight, bias, root, grad):
    nodes, width = own.shape
    half = jax.ShapeDtypeStruct((width // 2, width + 128), bf16)
    square = jax.ShapeDtypeStruct((nodes, width), bf16)
    vmem = pl.BlockSpec(memory_space=pltpu.VMEM)
    return pl.pallas_call(
        forward_kernel,
        in_specs=[pl.BlockSpec(memory_space=pltpu.SMEM)] + [vmem] * 9,
        out_specs=[vmem] * 6,
        out_shape=[square, half, half, square, square, square],
        scratch_shapes=[pltpu.VMEM((nodes, width), bf16)] * 2,
        compiler_params=pltpu.CompilerParams(vmem_limit_bytes=VMEM_LIMIT),
        cost_estimate=pl.CostEstimate(flops=10**9, bytes_accessed=10**7, transcendentals=0),
        name="forward",
    )(core, adj, edge, own, near, far, weight, bias, root, grad)


def spread_kernel(blocks, out):
    count = blocks.shape[0]
    total = blocks[0].astype(f32)
    for i in range(1, count):
        total += blocks[i].astype(f32)
    total = total.astype(bf16)
    copies, rows = out.shape[0], out.shape[1]
    each = copies * rows // blocks.shape[1]
    for i in range(copies):
        first = i // each * rows
        out[i] = total[first : first + rows]


def spread(blocks, pieces, copies):
    _, rows, width = blocks.shape
    vmem = pl.BlockSpec(memory_space=pltpu.VMEM)
    return pl.pallas_call(
        spread_kernel,
        in_specs=[vmem],
        out_specs=vmem,
        out_shape=jax.ShapeDtypeStruct((pieces * copies, rows // pieces, width), bf16),
        compiler_params=pltpu.CompilerParams(vmem_limit_bytes=VMEM_LIMIT),
        cost_estimate=pl.CostEstimate(flops=10**6, bytes_accessed=10**6, transcendentals=0),
        name="spread",
    )(blocks)


def halves_kernel(high_ref, blocks, sent, kept):
    count = blocks.shape[0]
    rows = sent.shape[0]
    for half, out_type in ((1 - high_ref[0], "sent"), (high_ref[0], "kept")):
        r = pl.ds(pl.multiple_of(half * rows, rows), rows)
        total = blocks[0, r, :].astype(f32)
        for i in range(1, count):
            total += blocks[i, r, :].astype(f32)
        if out_type == "sent":
            sent[...] = total.astype(bf16)
        else:
            kept[...] = total


def halves(high, blocks):
    _, rows, width = blocks.shape
    vmem = pl.BlockSpec(memory_space=pltpu.VMEM)
    return pl.pallas_call(
        halves_kernel,
        in_specs=[pl.BlockSpec(memory_space=pltpu.SMEM), vmem],
        out_specs=[vmem] * 2,
        out_shape=[
            jax.ShapeDtypeStruct((rows // 2, width), bf16),
            jax.ShapeDtypeStruct((rows // 2, width), f32),
        ],
        compiler_params=pltpu.CompilerParams(vmem_limit_bytes=VMEM_LIMIT),
        cost_estimate=pl.CostEstimate(flops=10**6, bytes_accessed=10**6, transcendentals=0),
        name="halves",
    )(high, blocks)


def merge_kernel(kept, pair, out):
    total = (kept[...] + pair[...].astype(f32)).astype(bf16)
    for i in range(out.shape[0]):
        out[i] = total


def merge(kept, pair, copies):
    vmem = pl.BlockSpec(memory_space=pltpu.VMEM)
    return pl.pallas_call(
        merge_kernel,
        in_specs=[vmem] * 2,
        out_specs=vmem,
        out_shape=jax.ShapeDtypeStruct((copies, *kept.shape), bf16),
        compiler_params=pltpu.CompilerParams(vmem_limit_bytes=VMEM_LIMIT),
        cost_estimate=pl.CostEstimate(flops=10**6, bytes_accessed=10**6, transcendentals=0),
        name="merge",
    )(kept, pair)


def last_sum_kernel(scale, blocks, out, bias):
    count, rows, width = blocks.shape
    total = blocks[0].astype(f32)
    for i in range(1, count):
        total += blocks[i].astype(f32)
    total = total * scale
    wide = out.shape[1]
    out[...] = total[:, 0:wide]
    column = total[:, wide:width]
    row = lax.broadcasted_iota(jnp.int32, column.shape, 0)
    lane = lax.broadcasted_iota(jnp.int32, column.shape, 1)
    flat = jnp.sum(jnp.where(row == lane, column, 0.0), axis=0, keepdims=True)
    bias[...] = flat[:, 0:rows]


def last_sum(blocks, scale):
    _, rows, width = blocks.shape
    vmem = pl.BlockSpec(memory_space=pltpu.VMEM)
    return pl.pallas_call(
        lambda *refs: last_sum_kernel(scale, *refs),
        in_specs=[vmem],
        out_specs=[vmem] * 2,
        out_shape=[
            jax.ShapeDtypeStruct((rows, width - 128), f32),
            jax.ShapeDtypeStruct((1, rows), f32),
        ],
        compiler_params=pltpu.CompilerParams(vmem_limit_bytes=VMEM_LIMIT),
        cost_estimate=pl.CostEstimate(flops=10**6, bytes_accessed=10**6, transcendentals=0),
        name="last_sum",
    )(blocks)


def own_part_kernel(adj, scaled, out):
    rows = 128
    for first in range(0, out.shape[0], rows):
        out[first : first + rows, :] = rows_dot(adj[first : first + rows, :], scaled[...])


def own_part(adj, scaled):
    vmem = pl.BlockSpec(memory_space=pltpu.VMEM)
    return pl.pallas_call(
        own_part_kernel,
        in_specs=[vmem] * 2,
        out_specs=vmem,
        out_shape=jax.ShapeDtypeStruct(scaled.shape, f32),
        compiler_params=pltpu.CompilerParams(vmem_limit_bytes=VMEM_LIMIT),
        cost_estimate=pl.CostEstimate(flops=10**12, bytes_accessed=10**9, transcendentals=0),
        name="own_part",
    )(adj, scaled)


def final_kernel(part_own, from_near, from_far, root, weight, out):
    nodes = out.shape[0]
    rows = 128
    for first in range(0, nodes, rows):
        r = pl.ds(first, rows)
        total = part_own[r, :] + from_near[r, :].astype(f32) + from_far[r, :].astype(f32)
        grad_proj = (root[r, :] * total).astype(bf16)
        out[r, :] = lax.dot_general(
            grad_proj, weight[...], (((1,), (1,)), ((), ())), preferred_element_type=f32
        ).astype(bf16)


def final(part_own, from_near, from_far, root, weight):
    vmem = pl.BlockSpec(memory_space=pltpu.VMEM)
    return pl.pallas_call(
        final_kernel,
        in_specs=[vmem] * 5,
        out_specs=vmem,
        out_shape=jax.ShapeDtypeStruct(part_own.shape, bf16),
        cost_estimate=pl.CostEstimate(flops=10**8, bytes_accessed=10**6, transcendentals=0),
        compiler_params=pltpu.CompilerParams(vmem_limit_bytes=VMEM_LIMIT),
        name="final",
    )(part_own, from_near, from_far, root, weight)


def local(features, weight, layer_bias, block_cols, neighbours, row_counts, out_grad):
    nodes, width = features.shape
    tile_count = block_cols.shape[0]
    devices = lax.axis_size(NODE)
    all_tiles = tile_count * devices
    normaliser = 1.0 / math.sqrt(nodes * devices)
    window_start = (lax.axis_index(NODE) - 1) * tile_count
    local_slot = jnp.mod(block_cols - window_start, all_tiles)
    group = local_slot // tile_count
    even = lax.axis_index(NODE) % 2 == 0
    local_slot = jnp.where(even, local_slot + 2 * (1 - group) * tile_count, local_slot)
    counts = row_counts[:, None]
    root = lax.rsqrt(1.0 + counts.astype(f32))
    own = (features.astype(f32) * root).astype(bf16)
    far = permute(own, NODE, far_partner)
    near = permute(own, NODE, near_partner)
    adj, edge, own_t = build_adjacency(local_slot, neighbours, counts)
    core = lax.axis_index("core").astype(jnp.int32).reshape(1)
    hidden, wsend, wkeep, scaled, part_near, part_far = forward(
        core, adj, edge, own, near, far, weight, layer_bias[None, :], root, out_grad
    )
    got = permute(wsend, "core", lambda i: i ^ 1)
    from_near = permute(part_near, NODE, near_partner)
    ny, nx, nzl = (lax.axis_size(n) for n in ("y", "x", "zl"))
    chip = (wkeep.astype(f32) + got.astype(f32)).astype(bf16)
    from_far = permute(part_far, NODE, far_partner)
    blocks = lax.all_to_all(chip.reshape(ny, -1, width + 128), "y", 0, 0)
    own_t, from_near = lax.optimization_barrier((own_t, from_near))
    part_own = own_part(own_t, scaled)
    blocks, part_own = lax.optimization_barrier((blocks, part_own))
    blocks = lax.all_to_all(spread(blocks, 1, nx), "x", 0, 0)
    high = lax.axis_index("zh").astype(jnp.int32).reshape(1)
    sent, kept = halves(high, blocks)
    pair = permute(sent, ("zh", "zl"), lambda i: -1 - i)
    blocks = merge(kept, pair, nzl)
    blocks, from_far = lax.optimization_barrier((blocks, from_far))
    blocks = lax.all_to_all(blocks, "zl", 0, 0)
    weight_grad, bias_grad = last_sum(blocks, normaliser)
    input_grad = final(part_own, from_near, from_far, root, weight)
    return (hidden, input_grad, weight_grad, bias_grad[0])


def solution(mesh):
    wide = Mesh(mesh.devices.reshape(SIZES), AXES)
    row = P(NODE, None)
    in_specs = (row, P(), P(), row, row, P(NODE), row)
    shares = ("y", "zh", "core")
    out_specs = (row, row, P(shares, None), P(shares))
    return jax.shard_map(local, mesh=wide, in_specs=in_specs, out_specs=out_specs, check_vma=False)
```
